32 devices in a mesh: groups: 2 (over y), section: 4 (over z), dp: 4 (over x, core).
Axes of the slice: x: 2, y: 2, z: 4, core: 2. Of those that a mesh axis runs over, the one named last changes fastest.
Arguments:
- stream_in: bfloat16 [1152, 3072], P(('groups', 'dp')), parts along dimension 0, may hold values from -6 to 6
- out_grad: bfloat16 [1152, 3072], P(('groups', 'dp')), parts along dimension 0, may hold values from -6 to 6
- mask_blocks: int32 [24, 3, 3], P(('groups', 'dp')), parts along dimension 0, may hold values from 0 to 2, as said below
- norm_gain: float32 [4, 3072], P('section'), may hold values from 0.4 to 1.6
- w_joined: bfloat16 [4, 3072, 1664], P('section', 'dp'), may hold values from -0.109375 to 0.109375
- w_out: bfloat16 [4, 1536, 3072], P('section', 'dp'), may hold values from -0.15625 to 0.15625
Outputs:
- grad_joined: float32 [8, 3072, 1664], P(('groups', 'section'), 'dp'), parts along dimension 0
- grad_out: float32 [8, 1536, 3072], P(('groups', 'section'), 'dp'), parts along dimension 0
- gain_grad: float32 [8, 3072], P(('groups', 'section')), parts along dimension 0
The draws below stay inside these ranges and needn't reach their ends.
There are 2 independent parts, one for each index of `groups`. The reference program is written for one: setup_inputs(seed, part) draws one part's arguments, and reference() takes and returns one part's arrays. A program takes and returns all parts, laid end to end along the dimension named above; an argument that names none is the same for every part. Nothing has to cross between parts.
Inputs may be any that keep to these rules, and one draw needn't show every extreme that they name: `mask_blocks`: entry 0 of the list of query block i is i itself.
All inputs are finite; a program needn't handle non-finite values.
Results may differ from the reference program's by a relative error of at most 0.024.
Values may be sent and summed in bfloat16 or wider, within the bound.
A program may use at most 128 MiB of HBM per device.

```python
import jax
import jax.numpy as jnp
from jax import lax

MODEL_DIM = 3072
NUM_HEADS = 24
HEAD_DIM = 64
MICRO_LEN = 48
BLOCK_LEN = 16
INNER_DIM = 1536
JOINED_DIM = 1664
NUM_BLOCKS = 3
SECTIONS = 4
MICRO_ALL = 12
TOKENS = 576
N_DP = 4


def draw_mask_blocks(key, part):
    base = jax.random.fold_in(key, 17)
    side_key, stripe_key = jax.random.split(base)
    own_block = jnp.broadcast_to(jnp.arange(NUM_BLOCKS, dtype=jnp.int32)[None, :], (MICRO_ALL, NUM_BLOCKS))
    side_step = jax.random.randint(side_key, (MICRO_ALL, NUM_BLOCKS), 0, 2).astype(jnp.int32) * 2 - 1
    near_block = jnp.clip(own_block + side_step, 0, NUM_BLOCKS - 1)
    stripe_block = jax.random.randint(stripe_key, (MICRO_ALL, NUM_BLOCKS), 0, NUM_BLOCKS).astype(jnp.int32)
    return jnp.stack([own_block, near_block, stripe_block], axis=-1).astype(jnp.int32)


def shard_levels(own_key, extent, cuts, smallest, top_value):
    def one(dim, blocks):
        heights = jax.random.uniform(jax.random.fold_in(jax.random.fold_in(own_key, 6), dim), (blocks,), jnp.float32, smallest / len(cuts), top_value / len(cuts))
        return jnp.repeat(jnp.exp(heights), extent[dim] // blocks).reshape((-1,) + (1,) * (len(extent) - dim - 1))

    factor_of = one(*cuts[0])
    for cut in cuts[1:]:
        factor_of = factor_of * one(*cut)
    return factor_of


def noise(key, dims, deviation, limit, pieces=(), held_as=jnp.bfloat16):
    values = jax.random.normal(key, dims, jnp.float32) * deviation
    if len(pieces) > 0:
        values = shard_levels(key, dims, pieces, -0.22, 0.18) * values
    return jnp.clip(values, min=-limit, max=limit).astype(held_as)


def setup_inputs(seed: int = 0, part: int = 0) -> dict:
    key_list = jax.random.split(jax.random.key(seed), 7)
    part_splits = jax.random.split(jax.random.fold_in(key_list[6], part), 7)
    return {
        "stream_in": noise(part_splits[0], (TOKENS, MODEL_DIM), 1.0, 6.0, ((0, 4),)),
        "out_grad": noise(part_splits[1], (TOKENS, MODEL_DIM), 1.0, 6.0, ((0, 4),)),
        "mask_blocks": draw_mask_blocks(jax.random.fold_in(jax.random.fold_in(key_list[6], part), 71), part),
        "norm_gain": jnp.clip(1.0 + 0.12 * jax.random.normal(key_list[3], (SECTIONS, MODEL_DIM), jnp.float32), 0.4, 1.6),
        "w_joined": noise(key_list[4], (SECTIONS, MODEL_DIM, JOINED_DIM), MODEL_DIM ** -0.5, 0.109375, ((0, 4), (1, 4))),
        "w_out": noise(key_list[5], (SECTIONS, INNER_DIM, MODEL_DIM), INNER_DIM ** -0.5, 0.15625, ((0, 4), (1, 4))),
    }


EPSILON = 1e-05

def allowed_tokens(links, block_len):
    count = links.shape[1]
    block_hits = links[:, :, :, None] == jnp.arange(count, dtype=jnp.int32)[None, None, None, :]
    blocks = jnp.any(block_hits, axis=2)
    return jnp.repeat(jnp.repeat(blocks, block_len, axis=1), block_len, axis=2)

def normalize(stream, gain_row):
    stream_wide = stream.astype(jnp.float32)
    inv_rms = lax.rsqrt(lax.optimization_barrier(jnp.mean(stream_wide * stream_wide, axis=-1, keepdims=True)) + EPSILON)
    normed = (stream_wide * inv_rms * gain_row).astype(jnp.bfloat16)
    return (stream_wide, inv_rms, normed)

def project(normed, weight):
    batch_size, length, model_width = normed.shape
    flat = jnp.dot(normed.reshape(-1, model_width), weight, preferred_element_type=jnp.float32)
    return flat.astype(jnp.bfloat16).reshape(batch_size, length, weight.shape[1])

def attend(joined_rows, allowed):
    batch_size, length, _ = joined_rows.shape
    inner_width = NUM_HEADS * HEAD_DIM
    queries = joined_rows[:, :, :inner_width].reshape(batch_size, length, NUM_HEADS, HEAD_DIM)
    key_rows = joined_rows[:, :, inner_width:inner_width + HEAD_DIM]
    values = joined_rows[:, :, inner_width + HEAD_DIM:]
    scores = jnp.einsum('bihd,bjd->bhij', queries.astype(jnp.float32), key_rows.astype(jnp.float32)) * HEAD_DIM ** (-0.5)
    scores = jnp.where(allowed[:, None], scores, -1e+30)
    row_max = lax.optimization_barrier(jnp.max(scores, axis=-1, keepdims=True))
    exp_scores = jnp.exp(scores - row_max)
    attn_probs = exp_scores / lax.optimization_barrier(jnp.sum(exp_scores, axis=-1, keepdims=True))
    probs_half = attn_probs.astype(jnp.bfloat16)
    mixed_heads = jnp.einsum('bhij,bjd->bihd', probs_half.astype(jnp.float32), values.astype(jnp.float32))
    mixed_heads = mixed_heads.astype(jnp.bfloat16).reshape(batch_size, length, inner_width)
    return (queries, key_rows, values, attn_probs, probs_half, mixed_heads)

def layer_forward(stream, gain_row, w_joined, w_out, allowed):
    stream_wide, inv_rms, normed = normalize(stream, gain_row)
    joined_rows = project(normed, w_joined)
    mixed_heads = attend(joined_rows, allowed)[5]
    batch_size, length, model_width = stream.shape
    update = jnp.dot(mixed_heads.reshape(-1, mixed_heads.shape[2]), w_out, preferred_element_type=jnp.float32)
    return (stream_wide + update.reshape(batch_size, length, model_width)).astype(jnp.bfloat16)

def layer_backward(stream, gain_row, joined_rows, w_joined, w_out, allowed, upstream):
    stream_wide, inv_rms, normed = normalize(stream, gain_row)
    queries, key_rows, values, attn_probs, probs_half, mixed_heads = attend(joined_rows, allowed)
    batch_size, length, model_width = stream.shape
    inner_width = NUM_HEADS * HEAD_DIM
    grad_mixed = lax.dot_general(upstream.reshape(-1, model_width), w_out, (((1,), (1,)), ((), ())), preferred_element_type=jnp.float32)
    grad_mixed = grad_mixed.astype(jnp.bfloat16).reshape(batch_size, length, NUM_HEADS, HEAD_DIM)
    grad_probs = jnp.einsum('bihd,bjd->bhij', grad_mixed.astype(jnp.float32), values.astype(jnp.float32))
    grad_values = jnp.einsum('bhij,bihd->bjd', probs_half.astype(jnp.float32), grad_mixed.astype(jnp.float32))
    inner_sum = lax.optimization_barrier(jnp.sum(attn_probs * grad_probs, axis=-1, keepdims=True))
    grad_scores = (attn_probs * (grad_probs - inner_sum) * HEAD_DIM ** (-0.5)).astype(jnp.bfloat16)
    grad_queries = jnp.einsum('bhij,bjd->bihd', grad_scores.astype(jnp.float32), key_rows.astype(jnp.float32))
    grad_keys = jnp.einsum('bhij,bihd->bjd', grad_scores.astype(jnp.float32), queries.astype(jnp.float32))
    grad_joined_rows = jnp.concatenate([grad_queries.reshape(batch_size, length, inner_width), grad_keys, grad_values], axis=-1).astype(jnp.bfloat16)
    grad_normed = lax.dot_general(grad_joined_rows.reshape(-1, grad_joined_rows.shape[2]), w_joined, (((1,), (1,)), ((), ())), preferred_element_type=jnp.float32)
    grad_normed = grad_normed.reshape(batch_size, length, model_width)
    gained = grad_normed * gain_row
    grad_stream = inv_rms * gained - stream_wide * inv_rms ** 3 * lax.optimization_barrier(jnp.mean(stream_wide * gained, axis=-1, keepdims=True))
    down_grad = (upstream.astype(jnp.float32) + grad_stream).astype(jnp.bfloat16)
    gain_part = lax.optimization_barrier(jnp.sum((grad_normed * stream_wide * inv_rms).reshape(-1, model_width), axis=0))
    return (down_grad, normed, grad_joined_rows, mixed_heads, gain_part)

def replica_sum(left, right):
    left_rows = left.reshape(N_DP, -1, left.shape[-1]).astype(jnp.float32)
    right_rows = right.reshape(N_DP, -1, right.shape[-1]).astype(jnp.float32)
    partial_sums = jnp.einsum('rtd,rtc->rdc', left_rows, right_rows)
    rounded = lax.optimization_barrier(partial_sums.astype(jnp.bfloat16))
    return lax.optimization_barrier(jnp.sum(rounded.astype(jnp.float32), axis=0))

def reference(stream_in, out_grad, mask_blocks, norm_gain, w_joined, w_out):
    allowed = allowed_tokens(mask_blocks, BLOCK_LEN)
    micro_count = mask_blocks.shape[0]
    model_width = stream_in.shape[1]
    current = stream_in.reshape(micro_count, MICRO_LEN, model_width)
    inputs_kept = []
    for section_index in range(SECTIONS):
        inputs_kept.append(current)
        current = layer_forward(current, norm_gain[section_index], w_joined[section_index], w_out[section_index], allowed)
    upstream = out_grad.reshape(micro_count, MICRO_LEN, model_width)
    joined_list = [None] * SECTIONS
    out_list = [None] * SECTIONS
    gain_list = [None] * SECTIONS
    for section_index in reversed(range(SECTIONS)):
        source = inputs_kept[section_index]
        normed = normalize(source, norm_gain[section_index])[2]
        joined_rows = project(normed, w_joined[section_index])
        down_grad, normed, grad_joined_rows, mixed_heads, gain_part = layer_backward(source, norm_gain[section_index], joined_rows, w_joined[section_index], w_out[section_index], allowed, upstream)
        joined_list[section_index] = replica_sum(normed, grad_joined_rows)
        out_list[section_index] = replica_sum(mixed_heads, upstream)
        gain_list[section_index] = gain_part
        upstream = down_grad
    return (jnp.stack(joined_list), jnp.stack(out_list), jnp.stack(gain_list))
```

```python
import jax
import jax.numpy as jnp
from jax import lax
from jax.sharding import PartitionSpec as P

NUM_HEADS = 24
HEAD_DIM = 64
BLOCK_LEN = 16


EPSILON = 1e-05


def from_behind(value, axis, steps):
    count = lax.axis_size(axis)
    initial, last = (max(0, -steps), min(count, count - steps))
    return lax.ppermute(value, axis, [(source, source + steps) for source in range(initial, last)])


def allowed_tokens(links, block_len):
    count = links.shape[1]
    block_hits = links[:, :, :, None] == jnp.arange(count, dtype=jnp.int32)[None, None, None, :]
    blocks = jnp.any(block_hits, axis=2)
    return jnp.repeat(jnp.repeat(blocks, block_len, axis=1), block_len, axis=2)


def normalize(stream, gain_row):
    stream_wide = stream.astype(jnp.float32)
    inv_rms = lax.rsqrt(jnp.mean(stream_wide * stream_wide, axis=-1, keepdims=True) + EPSILON)
    normed = (stream_wide * inv_rms * gain_row).astype(jnp.bfloat16)
    return (stream_wide, inv_rms, normed)


def project(normed, weight):
    batch_size, length, model_width = normed.shape
    flat = jnp.dot(normed.reshape(-1, model_width), weight, preferred_element_type=jnp.float32)
    return flat.astype(jnp.bfloat16).reshape(batch_size, length, weight.shape[1])


def attend(joined_rows, allowed):
    batch_size, length, _ = joined_rows.shape
    inner_width = NUM_HEADS * HEAD_DIM
    queries = joined_rows[:, :, :inner_width].reshape(batch_size, length, NUM_HEADS, HEAD_DIM)
    key_rows = joined_rows[:, :, inner_width : inner_width + HEAD_DIM]
    values = joined_rows[:, :, inner_width + HEAD_DIM :]
    scores = jnp.einsum(
        "bihd,bjd->bhij", queries, key_rows, preferred_element_type=jnp.float32
    ) * HEAD_DIM ** (-0.5)
    scores = jnp.where(allowed[:, None], scores, -1e30)
    row_max = jnp.max(scores, axis=-1, keepdims=True)
    exp_scores = jnp.exp(scores - row_max)
    attn_probs = exp_scores / jnp.sum(exp_scores, axis=-1, keepdims=True)
    probs_half = attn_probs.astype(jnp.bfloat16)
    mixed_heads = jnp.einsum(
        "bhij,bjd->bihd", probs_half, values, preferred_element_type=jnp.float32
    )
    mixed_heads = mixed_heads.astype(jnp.bfloat16).reshape(batch_size, length, inner_width)
    return (queries, key_rows, values, attn_probs, probs_half, mixed_heads)


def layer_forward(stream, gain_row, w_joined, w_out, allowed):
    stream_wide, inv_rms, normed = normalize(stream, gain_row)
    joined_rows = project(normed, w_joined)
    _, _, _, attn_probs, _, mixed_heads = attend(joined_rows, allowed)
    batch_size, length, model_width = stream.shape
    update = jnp.dot(
        mixed_heads.reshape(-1, mixed_heads.shape[2]), w_out, preferred_element_type=jnp.float32
    )
    result = (stream_wide + update.reshape(batch_size, length, model_width)).astype(jnp.bfloat16)
    return (result, normed, joined_rows, attn_probs, mixed_heads)


def layer_backward(stream, gain_row, joined_rows, attn_probs, w_joined, w_out, upstream):
    batch_size, length, model_width = stream.shape
    inner_width = NUM_HEADS * HEAD_DIM
    stream_wide = stream.astype(jnp.float32)
    inv_rms = lax.rsqrt(jnp.mean(stream_wide * stream_wide, axis=-1, keepdims=True) + EPSILON)
    queries = joined_rows[:, :, :inner_width].reshape(batch_size, length, NUM_HEADS, HEAD_DIM)
    key_rows = joined_rows[:, :, inner_width : inner_width + HEAD_DIM]
    values = joined_rows[:, :, inner_width + HEAD_DIM :]
    probs_half = attn_probs.astype(jnp.bfloat16)
    grad_mixed = lax.dot_general(
        upstream.reshape(-1, model_width),
        w_out,
        (((1,), (1,)), ((), ())),
        preferred_element_type=jnp.float32,
    )
    grad_mixed = grad_mixed.astype(jnp.bfloat16).reshape(batch_size, length, NUM_HEADS, HEAD_DIM)
    grad_probs = jnp.einsum(
        "bihd,bjd->bhij", grad_mixed, values, preferred_element_type=jnp.float32
    )
    grad_values = jnp.einsum(
        "bhij,bihd->bjd", probs_half, grad_mixed, preferred_element_type=jnp.float32
    )
    inner_sum = jnp.sum(attn_probs * grad_probs, axis=-1, keepdims=True)
    grad_scores = (attn_probs * (grad_probs - inner_sum) * HEAD_DIM ** (-0.5)).astype(jnp.bfloat16)
    grad_queries = jnp.einsum(
        "bhij,bjd->bihd", grad_scores, key_rows, preferred_element_type=jnp.float32
    )
    grad_keys = jnp.einsum(
        "bhij,bihd->bjd", grad_scores, queries, preferred_element_type=jnp.float32
    )
    grad_joined_rows = jnp.concatenate(
        [grad_queries.reshape(batch_size, length, inner_width), grad_keys, grad_values], axis=-1
    ).astype(jnp.bfloat16)
    grad_normed = lax.dot_general(
        grad_joined_rows.reshape(-1, grad_joined_rows.shape[2]),
        w_joined,
        (((1,), (1,)), ((), ())),
        preferred_element_type=jnp.float32,
    )
    grad_normed = grad_normed.reshape(batch_size, length, model_width)
    gained = grad_normed * gain_row
    grad_stream = inv_rms * gained - stream_wide * inv_rms**3 * jnp.mean(
        stream_wide * gained, axis=-1, keepdims=True
    )
    down_grad = (upstream.astype(jnp.float32) + grad_stream).astype(jnp.bfloat16)
    gain_part = jnp.sum((grad_normed * stream_wide * inv_rms).reshape(-1, model_width), axis=0)
    return (down_grad, grad_joined_rows, gain_part)


def pick(stack, index):
    return lax.dynamic_index_in_dim(stack, index, 0, keepdims=False)


def gather_weights(w_joined, w_out):
    return (
        lax.all_gather(w_joined[0], "dp", axis=0, tiled=True),
        lax.all_gather(w_out[0], "dp", axis=0, tiled=True),
    )


def share_columns(rows):
    n = lax.axis_size("dp")
    me = lax.axis_index("dp")
    slots, length, total = rows.shape
    width = total // n
    taken = jnp.zeros((slots, n, length, width), rows.dtype)
    for shift in range(n):
        target = lax.rem(me + shift, n)
        piece = lax.dynamic_slice_in_dim(rows, target * width, width, 2)
        if shift:
            piece = lax.ppermute(piece, "dp", [(i, (i + shift) % n) for i in range(n)])
        source = lax.rem(me + n - shift, n)
        taken = lax.dynamic_update_slice_in_dim(taken, piece[:, None], source, 1)
    return taken


def body(stream_in, out_grad, mask_blocks, norm_gain, w_joined, w_out):
    full_joined, full_out = gather_weights(w_joined, w_out)
    gain_row = norm_gain[0]
    sections = lax.axis_size("section")
    section_index = lax.axis_index("section")
    micro_count = mask_blocks.shape[0]
    model_width = stream_in.shape[1]
    length = stream_in.shape[0] // micro_count
    inputs = stream_in.reshape(micro_count, 1, length, model_width)
    upstreams = out_grad.reshape(micro_count, 1, length, model_width)
    allowed = allowed_tokens(mask_blocks, BLOCK_LEN).reshape(micro_count, 1, length, length)
    step_count = micro_count + sections - 1

    def forward_step(step, state):
        incoming, kept = state
        slot = step - section_index
        active = jnp.logical_and(slot >= 0, slot < micro_count)
        group_index = jnp.clip(slot, 0, micro_count - 1)
        source = jnp.where(section_index == 0, pick(inputs, group_index), incoming)
        result, normed, joined_rows, attn_probs, mixed_heads = layer_forward(
            source, gain_row, full_joined, full_out, pick(allowed, group_index)
        )
        place = jnp.where(active, group_index, micro_count)
        values = (source, joined_rows, attn_probs, normed, mixed_heads)
        kept = tuple(
            lax.dynamic_update_index_in_dim(store, value, place, 0)
            for store, value in zip(kept, values)
        )
        return (from_behind(result, "section", 1), kept)

    def store_of(*shape, dtype=jnp.bfloat16):
        return jnp.zeros((micro_count + 1,) + shape, dtype)

    joined_width = full_joined.shape[1]
    inner_width = full_out.shape[0]
    rest = jnp.zeros((1, length, model_width), jnp.bfloat16)
    kept = (
        store_of(1, length, model_width),
        store_of(1, length, joined_width),
        store_of(1, NUM_HEADS, length, length, dtype=jnp.float32),
        store_of(1, length, model_width),
        store_of(1, length, inner_width),
    )
    _, kept = lax.fori_loop(0, step_count, forward_step, (rest, kept))
    sources, joineds, probs, normeds, mixeds = kept
    columns_normed = share_columns(normeds[:micro_count, 0])
    columns_mixed = share_columns(mixeds[:micro_count, 0])

    behind = sections - 1 - section_index
    replicas = lax.axis_size("dp")

    def place_of(slot):
        return jnp.where(jnp.logical_and(slot >= 0, slot < micro_count), slot, micro_count)

    def backward_step(step, state):
        incoming, last_rows, all_upstream, all_joined, gain_sum = state
        slot = step - behind
        active = jnp.logical_and(slot >= 0, slot < micro_count)
        group_index = jnp.clip(slot, 0, micro_count - 1)
        upstream = jnp.where(section_index == sections - 1, pick(upstreams, group_index), incoming)
        shared_upstream = lax.all_gather(upstream[0], "dp", axis=0)
        shared_joined = lax.all_gather(last_rows, "dp", axis=0)
        down_grad, grad_joined_rows, gain_part = layer_backward(
            pick(sources, group_index),
            gain_row,
            pick(joineds, group_index),
            pick(probs, group_index),
            full_joined,
            full_out,
            upstream,
        )
        all_upstream = lax.dynamic_update_index_in_dim(
            all_upstream, shared_upstream, place_of(slot), 0
        )
        all_joined = lax.dynamic_update_index_in_dim(
            all_joined, shared_joined, place_of(slot - 1), 0
        )
        gain_sum = gain_sum + jnp.where(active, gain_part, 0.0)
        incoming = from_behind(down_grad, "section", -1)
        return (incoming, grad_joined_rows[0], all_upstream, all_joined, gain_sum)

    start_back = (
        rest,
        jnp.zeros((length, joined_width), jnp.bfloat16),
        store_of(replicas, length, model_width),
        store_of(replicas, length, joined_width),
        jnp.zeros((model_width,), jnp.float32),
    )
    _, last_rows, all_upstream, all_joined, gain_sum = lax.fori_loop(
        0, step_count, backward_step, start_back
    )
    all_joined = lax.dynamic_update_index_in_dim(
        all_joined,
        lax.all_gather(last_rows, "dp", axis=0),
        place_of(step_count - 1 - behind),
        0,
    )
    gain_total = jnp.sum(lax.all_gather(gain_sum, "dp", axis=0), axis=0)
    valid_upstream = all_upstream[:micro_count]
    valid_joined = all_joined[:micro_count]

    def flat(rows):
        return rows.reshape(-1, rows.shape[-1])

    over_rows = (((0,), (0,)), ((), ()))
    grad_joined = lax.dot_general(
        flat(columns_normed), flat(valid_joined), over_rows, preferred_element_type=jnp.float32
    )
    grad_output = lax.dot_general(
        flat(columns_mixed), flat(valid_upstream), over_rows, preferred_element_type=jnp.float32
    )
    return (grad_joined[None], grad_output[None], gain_total[None])


def solution(mesh):
    return jax.shard_map(
        body,
        mesh=mesh,
        in_specs=(
            P(("groups", "dp"), None),
            P(("groups", "dp"), None),
            P(("groups", "dp"), None, None),
            P("section", None),
            P("section", "dp", None),
            P("section", "dp", None),
        ),
        out_specs=(
            P(("groups", "section"), "dp", None),
            P(("groups", "section"), "dp", None),
            P(("groups", "section"), None),
        ),
        check_vma=False,
    )
```

```python
import functools

import jax
import jax.numpy as jnp
from jax import lax
from jax.experimental import pallas as pl
from jax.experimental.pallas import tpu as pltpu
from jax.sharding import PartitionSpec as P

NUM_HEADS = 24
HEAD_DIM = 64
BLOCK_LEN = 16


EPSILON = 1e-05


def from_behind(value, axis, steps):
    count = lax.axis_size(axis)
    initial, last = (max(0, -steps), min(count, count - steps))
    return lax.ppermute(value, axis, [(source, source + steps) for source in range(initial, last)])


def allowed_tokens(links, block_len):
    count = links.shape[1]
    block_hits = links[:, :, :, None] == jnp.arange(count, dtype=jnp.int32)[None, None, None, :]
    blocks = jnp.any(block_hits, axis=2)
    return jnp.repeat(jnp.repeat(blocks, block_len, axis=1), block_len, axis=2)


def normalize(stream, gain_row):
    stream_wide = stream.astype(jnp.float32)
    inv_rms = lax.rsqrt(jnp.mean(stream_wide * stream_wide, axis=-1, keepdims=True) + EPSILON)
    normed = (stream_wide * inv_rms * gain_row).astype(jnp.bfloat16)
    return (stream_wide, inv_rms, normed)


def project(normed, weight):
    batch_size, length, model_width = normed.shape
    flat = jnp.dot(normed.reshape(-1, model_width), weight, preferred_element_type=jnp.float32)
    return flat.astype(jnp.bfloat16).reshape(batch_size, length, weight.shape[1])


def attend(joined_rows, allowed):
    batch_size, length, _ = joined_rows.shape
    inner_width = NUM_HEADS * HEAD_DIM
    queries = joined_rows[:, :, :inner_width].reshape(batch_size, length, NUM_HEADS, HEAD_DIM)
    key_rows = joined_rows[:, :, inner_width : inner_width + HEAD_DIM]
    values = joined_rows[:, :, inner_width + HEAD_DIM :]
    scores = jnp.einsum(
        "bihd,bjd->bhij", queries, key_rows, preferred_element_type=jnp.float32
    ) * HEAD_DIM ** (-0.5)
    scores = jnp.where(allowed[:, None], scores, -1e30)
    row_max = jnp.max(scores, axis=-1, keepdims=True)
    exp_scores = jnp.exp(scores - row_max)
    attn_probs = exp_scores / jnp.sum(exp_scores, axis=-1, keepdims=True)
    probs_half = attn_probs.astype(jnp.bfloat16)
    mixed_heads = jnp.einsum(
        "bhij,bjd->bihd", probs_half, values, preferred_element_type=jnp.float32
    )
    mixed_heads = mixed_heads.astype(jnp.bfloat16).reshape(batch_size, length, inner_width)
    return (queries, key_rows, values, attn_probs, probs_half, mixed_heads)


def layer_forward(stream, gain_row, w_joined, w_out, allowed):
    stream_wide, inv_rms, normed = normalize(stream, gain_row)
    joined_rows = project(normed, w_joined)
    mixed_heads = attend(joined_rows, allowed)[5]
    batch_size, length, model_width = stream.shape
    update = jnp.dot(
        mixed_heads.reshape(-1, mixed_heads.shape[2]), w_out, preferred_element_type=jnp.float32
    )
    result = (stream_wide + update.reshape(batch_size, length, model_width)).astype(jnp.bfloat16)
    return (result, joined_rows)


def layer_backward(stream, gain_row, joined_rows, w_joined, w_out, allowed, upstream):
    stream_wide, inv_rms, normed = normalize(stream, gain_row)
    queries, key_rows, values, attn_probs, probs_half, mixed_heads = attend(joined_rows, allowed)
    batch_size, length, model_width = stream.shape
    inner_width = NUM_HEADS * HEAD_DIM
    grad_mixed = lax.dot_general(
        upstream.reshape(-1, model_width),
        w_out,
        (((1,), (1,)), ((), ())),
        preferred_element_type=jnp.float32,
    )
    grad_mixed = grad_mixed.astype(jnp.bfloat16).reshape(batch_size, length, NUM_HEADS, HEAD_DIM)
    grad_probs = jnp.einsum(
        "bihd,bjd->bhij", grad_mixed, values, preferred_element_type=jnp.float32
    )
    grad_values = jnp.einsum(
        "bhij,bihd->bjd", probs_half, grad_mixed, preferred_element_type=jnp.float32
    )
    inner_sum = jnp.sum(attn_probs * grad_probs, axis=-1, keepdims=True)
    grad_scores = (attn_probs * (grad_probs - inner_sum) * HEAD_DIM ** (-0.5)).astype(jnp.bfloat16)
    grad_queries = jnp.einsum(
        "bhij,bjd->bihd", grad_scores, key_rows, preferred_element_type=jnp.float32
    )
    grad_keys = jnp.einsum(
        "bhij,bihd->bjd", grad_scores, queries, preferred_element_type=jnp.float32
    )
    grad_joined_rows = jnp.concatenate(
        [grad_queries.reshape(batch_size, length, inner_width), grad_keys, grad_values], axis=-1
    ).astype(jnp.bfloat16)
    grad_normed = lax.dot_general(
        grad_joined_rows.reshape(-1, grad_joined_rows.shape[2]),
        w_joined,
        (((1,), (1,)), ((), ())),
        preferred_element_type=jnp.float32,
    )
    grad_normed = grad_normed.reshape(batch_size, length, model_width)
    gained = grad_normed * gain_row
    grad_stream = inv_rms * gained - stream_wide * inv_rms**3 * jnp.mean(
        stream_wide * gained, axis=-1, keepdims=True
    )
    down_grad = (upstream.astype(jnp.float32) + grad_stream).astype(jnp.bfloat16)
    gain_part = jnp.sum((grad_normed * stream_wide * inv_rms).reshape(-1, model_width), axis=0)
    return (down_grad, normed, grad_joined_rows, mixed_heads, gain_part)


def pass_forward(values):
    return from_behind(values, "section", 1)


def pass_backward(values):
    return from_behind(values, "section", -1)


CORES = 2
CHUNKS = 4


def gather_kernel(chips, groups, joined_ref, out_ref, full_joined, full_out, local_sems, *sems):
    send_x, recv_x, send_y, recv_y, send_own, recv_own, send_c, recv_c = sems
    me = lax.axis_index("dp")
    chip, core = me // CORES, lax.rem(me, CORES)
    group = lax.axis_index("groups")
    sibling = me + 1 - 2 * core
    pairs = ((joined_ref, full_joined), (out_ref, full_out))

    barrier = pltpu.get_barrier_semaphore()
    partners = [{"dp": sibling}]
    partners += [{"dp": lax.rem(chip + k, chips) * CORES + core} for k in range(1, chips)]
    partners += [{"groups": lax.rem(group + g, groups)} for g in range(1, groups)]
    for partner in partners:
        pl.semaphore_signal(
            barrier, inc=1, device_id=partner, device_id_type=pl.DeviceIdType.MESH
        )
    pl.semaphore_wait(barrier, len(partners))

    def remote(src, dst, send_sem, recv_sem, partner):
        return pltpu.make_async_remote_copy(
            src_ref=src,
            dst_ref=dst,
            send_sem=send_sem,
            recv_sem=recv_sem,
            device_id=partner,
            device_id_type=pl.DeviceIdType.MESH,
        )

    def span(w, owner, part, chunk):
        rows = pairs[w][0].shape[0]
        size = rows // (groups * CHUNKS)
        inside = (part * CHUNKS + chunk) * size
        return pl.ds(inside, size), pl.ds(owner * rows + inside, size)

    first = {}
    for w, (mine, full) in enumerate(pairs):
        for chunk in range(CHUNKS):
            for k in range(1, chips):
                here, there = span(w, me, group, chunk)
                copy = remote(
                    mine.at[here],
                    full.at[there],
                    send_x.at[w, chunk, k - 1],
                    recv_x.at[w, chunk, k - 1],
                    partners[k],
                )
                copy.start()
                first[w, chunk, k] = copy
    own, local = [], []
    for w, (mine, full) in enumerate(pairs):
        rows = mine.shape[0]
        place = full.at[pl.ds(me * rows, rows)]
        own.append(remote(mine, place, send_own.at[w], recv_own.at[w], partners[0]))
        own[-1].start()
        local.append(pltpu.make_async_copy(mine, place, local_sems.at[w]))
        local[-1].start()

    second, third = {}, []
    order = [
        (w, chunk, k) for w in range(2) for chunk in range(CHUNKS) for k in range(1, chips)
    ]

    def hand_over(w, chunk, k):
        owner = lax.rem(chip + chips - k, chips) * CORES + core
        for g in range(1, groups):
            second[w, chunk, k, g].wait_recv()
            part = lax.rem(group + groups - g, groups)
            _, place = span(w, owner, part, chunk)
            copy = remote(
                pairs[w][1].at[place],
                pairs[w][1].at[place],
                send_c.at[w, chunk, k - 1, g],
                recv_c.at[w, chunk, k - 1, g],
                partners[0],
            )
            copy.start()
            third.append(copy)

    for at, (w, chunk, k) in enumerate(order):
        first[w, chunk, k].wait_recv()
        owner = lax.rem(chip + chips - k, chips) * CORES + core
        _, place = span(w, owner, group, chunk)
        block = pairs[w][1].at[place]
        for g in range(1, groups):
            copy = remote(
                block,
                block,
                send_y.at[w, chunk, k - 1, g - 1],
                recv_y.at[w, chunk, k - 1, g - 1],
                partners[chips - 1 + g],
            )
            copy.start()
            second[w, chunk, k, g] = copy
        copy = remote(
            block,
            block,
            send_c.at[w, chunk, k - 1, 0],
            recv_c.at[w, chunk, k - 1, 0],
            partners[0],
        )
        copy.start()
        third.append(copy)
        if at:
            hand_over(*order[at - 1])
    hand_over(*order[-1])

    for copy in local:
        copy.wait()
    for copy in own:
        copy.wait()
    for copy in first.values():
        copy.wait_send()
    for copy in second.values():
        copy.wait_send()
    for copy in third:
        copy.wait()


def gather_weights(w_joined, w_out):
    replicas = lax.axis_size("dp")
    chips, groups = replicas // CORES, lax.axis_size("groups")
    shards = (w_joined[0], w_out[0])
    x_shape = (2, CHUNKS, chips - 1)
    dma = pltpu.SemaphoreType.DMA
    anywhere = pl.BlockSpec(memory_space=pl.ANY)
    return pl.pallas_call(
        functools.partial(gather_kernel, chips, groups),
        out_shape=[
            jax.ShapeDtypeStruct((replicas * each.shape[0], each.shape[1]), each.dtype)
            for each in shards
        ],
        in_specs=[anywhere] * 2,
        out_specs=[anywhere] * 2,
        scratch_shapes=[dma((2,)), dma(x_shape), dma(x_shape)]
        + [dma(x_shape + (groups - 1,))] * 2
        + [dma((2,))] * 2
        + [dma(x_shape + (groups,))] * 2,
        compiler_params=pltpu.CompilerParams(collective_id=0, has_side_effects=True),
    )(*shards)


def share_columns(rows):
    n = lax.axis_size("dp")
    me = lax.axis_index("dp")
    count, total = rows.shape
    width = total // n
    taken = jnp.zeros((n, count, width), rows.dtype)
    for shift in range(n):
        target = lax.rem(me + shift, n)
        piece = lax.dynamic_slice_in_dim(rows, target * width, width, 1)
        if shift:
            piece = lax.ppermute(piece, "dp", [(i, (i + shift) % n) for i in range(n)])
        source = lax.rem(me + n - shift, n)
        taken = lax.dynamic_update_slice_in_dim(taken, piece[None], source, 0)
    return taken.reshape(n * count, width)


def body(stream_in, out_grad, mask_blocks, norm_gain, w_joined, w_out):
    full_joined, full_out = gather_weights(w_joined, w_out)
    gain_row = norm_gain[0]
    sections = lax.axis_size("section")
    section_index = lax.axis_index("section")
    micro_count = mask_blocks.shape[0]
    model_width = stream_in.shape[1]
    length = stream_in.shape[0] // micro_count
    joined_width = full_joined.shape[1]
    inner_width = full_out.shape[0]
    per_group = micro_count // micro_count
    inputs = stream_in.reshape(micro_count, per_group, length, model_width)
    upstreams = out_grad.reshape(micro_count, per_group, length, model_width)
    allowed = allowed_tokens(mask_blocks, BLOCK_LEN).reshape(micro_count, per_group, length, length)
    step_count = micro_count + sections - 1
    keep_shape = (micro_count, per_group, length, joined_width)

    def forward_step(step_now, state_now):
        incoming, kept_inputs, kept_joined = state_now
        slot_index = step_now - section_index
        active = jnp.logical_and(slot_index >= 0, slot_index < micro_count)
        group_index = jnp.clip(slot_index, 0, micro_count - 1)
        source = jnp.where(section_index == 0, inputs[group_index], incoming)

        def forward_run(kept_pair):
            result, joined_rows = layer_forward(
                source, gain_row, full_joined, full_out, allowed[group_index]
            )
            new_inputs = lax.dynamic_update_index_in_dim(kept_pair[0], source, group_index, 0)
            new_joined = lax.dynamic_update_index_in_dim(kept_pair[1], joined_rows, group_index, 0)
            return (result, new_inputs, new_joined)

        def forward_rest(kept_pair):
            return (jnp.zeros_like(source), kept_pair[0], kept_pair[1])

        result, kept_inputs, kept_joined = lax.cond(
            active, forward_run, forward_rest, (kept_inputs, kept_joined)
        )
        return (pass_forward(result), kept_inputs, kept_joined)

    start_state = (
        jnp.zeros((per_group, length, model_width), jnp.bfloat16),
        jnp.zeros((micro_count, per_group, length, model_width), jnp.bfloat16),
        jnp.zeros(keep_shape, jnp.bfloat16),
    )
    _, kept_inputs, kept_joined = lax.fori_loop(0, step_count, forward_step, start_state)

    def backward_step(step_now, state_now):
        incoming, stores = state_now
        slot_index = step_now - (sections - 1 - section_index)
        active = jnp.logical_and(slot_index >= 0, slot_index < micro_count)
        group_index = jnp.clip(slot_index, 0, micro_count - 1)
        upstream = jnp.where(section_index == sections - 1, upstreams[group_index], incoming)

        def backward_run(store_now):
            source = kept_inputs[group_index]
            joined_rows = kept_joined[group_index]
            down_grad, normed, grad_joined_rows, mixed_heads, gain_part = layer_backward(
                source, gain_row, joined_rows, full_joined, full_out, allowed[group_index], upstream
            )
            new_store = (
                lax.dynamic_update_index_in_dim(store_now[0], normed, group_index, 0),
                lax.dynamic_update_index_in_dim(store_now[1], grad_joined_rows, group_index, 0),
                lax.dynamic_update_index_in_dim(store_now[2], mixed_heads, group_index, 0),
                lax.dynamic_update_index_in_dim(store_now[3], upstream, group_index, 0),
                store_now[4] + gain_part,
            )
            return (down_grad, new_store)

        def backward_rest(store_now):
            return (jnp.zeros_like(upstream), store_now)

        down_grad, stores = lax.cond(active, backward_run, backward_rest, stores)
        return (pass_backward(down_grad), stores)

    empty_stores = (
        jnp.zeros((micro_count, per_group, length, model_width), jnp.bfloat16),
        jnp.zeros((micro_count, per_group, length, joined_width), jnp.bfloat16),
        jnp.zeros((micro_count, per_group, length, inner_width), jnp.bfloat16),
        jnp.zeros((micro_count, per_group, length, model_width), jnp.bfloat16),
        jnp.zeros((model_width,), jnp.float32),
    )
    start_back = (jnp.zeros((per_group, length, model_width), jnp.bfloat16), empty_stores)
    _, stores = lax.fori_loop(0, step_count, backward_step, start_back)
    rows_normed = stores[0].reshape(-1, model_width)
    rows_joined = stores[1].reshape(-1, joined_width)
    rows_mixed = stores[2].reshape(-1, inner_width)
    rows_upstream = stores[3].reshape(-1, model_width)
    over_rows = (((0,), (0,)), ((), ()))
    gain_total = jnp.sum(lax.all_gather(stores[4], "dp", axis=0), axis=0)
    all_upstream = lax.all_gather(rows_upstream, "dp", axis=0, tiled=True)
    all_joined = lax.all_gather(rows_joined, "dp", axis=0, tiled=True)
    grad_output = lax.dot_general(
        share_columns(rows_mixed), all_upstream, over_rows, preferred_element_type=jnp.float32
    )
    grad_joined = lax.dot_general(
        share_columns(rows_normed), all_joined, over_rows, preferred_element_type=jnp.float32
    )
    return (grad_joined[None], grad_output[None], gain_total[None])


def solution(mesh):
    return jax.shard_map(
        body,
        mesh=mesh,
        in_specs=(
            P(("groups", "dp"), None),
            P(("groups", "dp"), None),
            P(("groups", "dp"), None, None),
            P("section", None),
            P("section", "dp", None),
            P("section", "dp", None),
        ),
        out_specs=(
            P(("groups", "section"), "dp", None),
            P(("groups", "section"), "dp", None),
            P(("groups", "section"), None),
        ),
        check_vma=False,
    )
```

```python
import functools

import jax
import jax.numpy as jnp
from jax import lax
from jax.experimental import pallas as pl
from jax.experimental.pallas import tpu as pltpu
from jax.sharding import PartitionSpec as P

NUM_HEADS = 24
HEAD_DIM = 64
BLOCK_LEN = 16


EPSILON = 1e-05


def from_behind(value, axis, steps):
    count = lax.axis_size(axis)
    initial, last = (max(0, -steps), min(count, count - steps))
    return lax.ppermute(value, axis, [(source, source + steps) for source in range(initial, last)])


def allowed_tokens(links, block_len):
    count = links.shape[1]
    block_hits = links[:, :, :, None] == jnp.arange(count, dtype=jnp.int32)[None, None, None, :]
    blocks = jnp.any(block_hits, axis=2)
    return jnp.repeat(jnp.repeat(blocks, block_len, axis=1), block_len, axis=2)


def normalize(stream, gain_row):
    stream_wide = stream.astype(jnp.float32)
    inv_rms = lax.rsqrt(jnp.mean(stream_wide * stream_wide, axis=-1, keepdims=True) + EPSILON)
    normed = (stream_wide * inv_rms * gain_row).astype(jnp.bfloat16)
    return (stream_wide, inv_rms, normed)


def project(normed, weight):
    batch_size, length, model_width = normed.shape
    flat = jnp.dot(normed.reshape(-1, model_width), weight, preferred_element_type=jnp.float32)
    return flat.astype(jnp.bfloat16).reshape(batch_size, length, weight.shape[1])


def attend(joined_rows, allowed):
    batch_size, length, _ = joined_rows.shape
    inner_width = NUM_HEADS * HEAD_DIM
    queries = joined_rows[:, :, :inner_width].reshape(batch_size, length, NUM_HEADS, HEAD_DIM)
    key_rows = joined_rows[:, :, inner_width : inner_width + HEAD_DIM]
    values = joined_rows[:, :, inner_width + HEAD_DIM :]
    scores = jnp.einsum(
        "bihd,bjd->bhij", queries, key_rows, preferred_element_type=jnp.float32
    ) * HEAD_DIM ** (-0.5)
    scores = jnp.where(allowed[:, None], scores, -1e30)
    row_max = jnp.max(scores, axis=-1, keepdims=True)
    exp_scores = jnp.exp(scores - row_max)
    attn_probs = exp_scores / jnp.sum(exp_scores, axis=-1, keepdims=True)
    probs_half = attn_probs.astype(jnp.bfloat16)
    mixed_heads = jnp.einsum(
        "bhij,bjd->bihd", probs_half, values, preferred_element_type=jnp.float32
    )
    mixed_heads = mixed_heads.astype(jnp.bfloat16).reshape(batch_size, length, inner_width)
    return (queries, key_rows, values, attn_probs, probs_half, mixed_heads)


def layer_forward(stream, gain_row, w_joined, w_out, allowed):
    stream_wide, inv_rms, normed = normalize(stream, gain_row)
    joined_rows = project(normed, w_joined)
    mixed_heads = attend(joined_rows, allowed)[5]
    batch_size, length, model_width = stream.shape
    update = jnp.dot(
        mixed_heads.reshape(-1, mixed_heads.shape[2]), w_out, preferred_element_type=jnp.float32
    )
    result = (stream_wide + update.reshape(batch_size, length, model_width)).astype(jnp.bfloat16)
    return (result, joined_rows)


def layer_backward(stream, gain_row, joined_rows, w_joined, w_out, allowed, upstream):
    stream_wide, inv_rms, normed = normalize(stream, gain_row)
    queries, key_rows, values, attn_probs, probs_half, mixed_heads = attend(joined_rows, allowed)
    batch_size, length, model_width = stream.shape
    inner_width = NUM_HEADS * HEAD_DIM
    grad_mixed = lax.dot_general(
        upstream.reshape(-1, model_width),
        w_out,
        (((1,), (1,)), ((), ())),
        preferred_element_type=jnp.float32,
    )
    grad_mixed = grad_mixed.astype(jnp.bfloat16).reshape(batch_size, length, NUM_HEADS, HEAD_DIM)
    grad_probs = jnp.einsum(
        "bihd,bjd->bhij", grad_mixed, values, preferred_element_type=jnp.float32
    )
    grad_values = jnp.einsum(
        "bhij,bihd->bjd", probs_half, grad_mixed, preferred_element_type=jnp.float32
    )
    inner_sum = jnp.sum(attn_probs * grad_probs, axis=-1, keepdims=True)
    grad_scores = (attn_probs * (grad_probs - inner_sum) * HEAD_DIM ** (-0.5)).astype(jnp.bfloat16)
    grad_queries = jnp.einsum(
        "bhij,bjd->bihd", grad_scores, key_rows, preferred_element_type=jnp.float32
    )
    grad_keys = jnp.einsum(
        "bhij,bihd->bjd", grad_scores, queries, preferred_element_type=jnp.float32
    )
    grad_joined_rows = jnp.concatenate(
        [grad_queries.reshape(batch_size, length, inner_width), grad_keys, grad_values], axis=-1
    ).astype(jnp.bfloat16)
    grad_normed = lax.dot_general(
        grad_joined_rows.reshape(-1, grad_joined_rows.shape[2]),
        w_joined,
        (((1,), (1,)), ((), ())),
        preferred_element_type=jnp.float32,
    )
    grad_normed = grad_normed.reshape(batch_size, length, model_width)
    gained = grad_normed * gain_row
    grad_stream = inv_rms * gained - stream_wide * inv_rms**3 * jnp.mean(
        stream_wide * gained, axis=-1, keepdims=True
    )
    down_grad = (upstream.astype(jnp.float32) + grad_stream).astype(jnp.bfloat16)
    gain_part = jnp.sum((grad_normed * stream_wide * inv_rms).reshape(-1, model_width), axis=0)
    return (down_grad, normed, grad_joined_rows, mixed_heads, gain_part)


def pass_forward(values):
    return from_behind(values, "section", 1)


def pass_backward(values):
    return from_behind(values, "section", -1)


CORES = 2
CHUNKS = 4


def gather_kernel(chips, groups, joined_ref, out_ref, full_joined, full_out, held_joined, held_out, *sems):
    load_sems, store_sems, send_x, recv_x, send_y, recv_y, send_own, recv_own, send_c, recv_c = sems
    me = lax.axis_index("dp")
    chip, core = me // CORES, lax.rem(me, CORES)
    group = lax.axis_index("groups")
    sibling = me + 1 - 2 * core
    pairs = ((joined_ref, full_joined), (out_ref, full_out))
    held = (held_joined, held_out)
    loads = [
        pltpu.make_async_copy(pairs[w][0], held[w], load_sems.at[w]) for w in range(2)
    ]
    for copy in loads:
        copy.start()

    barrier = pltpu.get_barrier_semaphore()
    partners = [{"dp": sibling}]
    partners += [{"dp": lax.rem(chip + k, chips) * CORES + core} for k in range(1, chips)]
    partners += [{"groups": lax.rem(group + g, groups)} for g in range(1, groups)]
    for partner in partners:
        pl.semaphore_signal(
            barrier, inc=1, device_id=partner, device_id_type=pl.DeviceIdType.MESH
        )
    pl.semaphore_wait(barrier, len(partners))

    def remote(src, dst, send_sem, recv_sem, partner):
        return pltpu.make_async_remote_copy(
            src_ref=src,
            dst_ref=dst,
            send_sem=send_sem,
            recv_sem=recv_sem,
            device_id=partner,
            device_id_type=pl.DeviceIdType.MESH,
        )

    def span(w, owner, part, chunk):
        rows = pairs[w][0].shape[0]
        size = rows // (groups * CHUNKS)
        inside = (part * CHUNKS + chunk) * size
        return pl.ds(inside, size), pl.ds(owner * rows + inside, size)

    first = {}
    for w, (mine, full) in enumerate(pairs):
        for chunk in range(CHUNKS):
            for k in range(1, chips):
                here, there = span(w, me, group, chunk)
                copy = remote(
                    mine.at[here],
                    full.at[there],
                    send_x.at[w, chunk, k - 1],
                    recv_x.at[w, chunk, k - 1],
                    partners[k],
                )
                copy.start()
                first[w, chunk, k] = copy
    own, local = [], []
    for w, (mine, full) in enumerate(pairs):
        rows = mine.shape[0]
        place = full.at[pl.ds(me * rows, rows)]
        own.append(remote(mine, place, send_own.at[w], recv_own.at[w], partners[0]))
        own[-1].start()
        loads[w].wait()
        local.append(pltpu.make_async_copy(held[w], place, store_sems.at[w]))
        local[-1].start()

    second, third = {}, []
    order = [
        (w, chunk, k) for w in range(2) for chunk in range(CHUNKS) for k in range(1, chips)
    ]

    def hand_over(w, chunk, k):
        owner = lax.rem(chip + chips - k, chips) * CORES + core
        for g in range(1, groups):
            second[w, chunk, k, g].wait_recv()
            part = lax.rem(group + groups - g, groups)
            _, place = span(w, owner, part, chunk)
            copy = remote(
                pairs[w][1].at[place],
                pairs[w][1].at[place],
                send_c.at[w, chunk, k - 1, g],
                recv_c.at[w, chunk, k - 1, g],
                partners[0],
            )
            copy.start()
            third.append(copy)

    for at, (w, chunk, k) in enumerate(order):
        first[w, chunk, k].wait_recv()
        owner = lax.rem(chip + chips - k, chips) * CORES + core
        _, place = span(w, owner, group, chunk)
        block = pairs[w][1].at[place]
        for g in range(1, groups):
            copy = remote(
                block,
                block,
                send_y.at[w, chunk, k - 1, g - 1],
                recv_y.at[w, chunk, k - 1, g - 1],
                partners[chips - 1 + g],
            )
            copy.start()
            second[w, chunk, k, g] = copy
        copy = remote(
            block,
            block,
            send_c.at[w, chunk, k - 1, 0],
            recv_c.at[w, chunk, k - 1, 0],
            partners[0],
        )
        copy.start()
        third.append(copy)
        if at:
            hand_over(*order[at - 1])
    hand_over(*order[-1])

    for copy in local:
        copy.wait()
    for copy in own:
        copy.wait()
    for copy in first.values():
        copy.wait_send()
    for copy in second.values():
        copy.wait_send()
    for copy in third:
        copy.wait()


def gather_weights(w_joined, w_out):
    replicas = lax.axis_size("dp")
    chips, groups = replicas // CORES, lax.axis_size("groups")
    shards = (w_joined[0], w_out[0])
    x_shape = (2, CHUNKS, chips - 1)
    dma = pltpu.SemaphoreType.DMA
    anywhere = pl.BlockSpec(memory_space=pl.ANY)
    return pl.pallas_call(
        functools.partial(gather_kernel, chips, groups),
        out_shape=[
            jax.ShapeDtypeStruct((replicas * each.shape[0], each.shape[1]), each.dtype)
            for each in shards
        ],
        in_specs=[anywhere] * 2,
        out_specs=[anywhere] * 2,
        scratch_shapes=[pltpu.VMEM(each.shape, each.dtype) for each in shards]
        + [dma((2,)), dma((2,)), dma(x_shape), dma(x_shape)]
        + [dma(x_shape + (groups - 1,))] * 2
        + [dma((2,))] * 2
        + [dma(x_shape + (groups,))] * 2,
        compiler_params=pltpu.CompilerParams(
            collective_id=0, has_side_effects=True, vmem_limit_bytes=16 << 20
        ),
    )(*shards)


def share_columns(rows):
    n = lax.axis_size("dp")
    me = lax.axis_index("dp")
    count, total = rows.shape
    width = total // n
    taken = jnp.zeros((n, count, width), rows.dtype)
    for shift in range(n):
        target = lax.rem(me + shift, n)
        piece = lax.dynamic_slice_in_dim(rows, target * width, width, 1)
        if shift:
            piece = lax.ppermute(piece, "dp", [(i, (i + shift) % n) for i in range(n)])
        source = lax.rem(me + n - shift, n)
        taken = lax.dynamic_update_slice_in_dim(taken, piece[None], source, 0)
    return taken.reshape(n * count, width)


def body(stream_in, out_grad, mask_blocks, norm_gain, w_joined, w_out):
    full_joined, full_out = gather_weights(w_joined, w_out)
    gain_row = norm_gain[0]
    sections = lax.axis_size("section")
    section_index = lax.axis_index("section")
    micro_count = mask_blocks.shape[0]
    model_width = stream_in.shape[1]
    length = stream_in.shape[0] // micro_count
    joined_width = full_joined.shape[1]
    inner_width = full_out.shape[0]
    per_group = micro_count // micro_count
    inputs = stream_in.reshape(micro_count, per_group, length, model_width)
    upstreams = out_grad.reshape(micro_count, per_group, length, model_width)
    allowed = allowed_tokens(mask_blocks, BLOCK_LEN).reshape(micro_count, per_group, length, length)
    step_count = micro_count + sections - 1
    keep_shape = (micro_count, per_group, length, joined_width)

    def forward_step(step_now, state_now):
        incoming, kept_inputs, kept_joined = state_now
        slot_index = step_now - section_index
        active = jnp.logical_and(slot_index >= 0, slot_index < micro_count)
        group_index = jnp.clip(slot_index, 0, micro_count - 1)
        source = jnp.where(section_index == 0, inputs[group_index], incoming)

        def forward_run(kept_pair):
            result, joined_rows = layer_forward(
                source, gain_row, full_joined, full_out, allowed[group_index]
            )
            new_inputs = lax.dynamic_update_index_in_dim(kept_pair[0], source, group_index, 0)
            new_joined = lax.dynamic_update_index_in_dim(kept_pair[1], joined_rows, group_index, 0)
            return (result, new_inputs, new_joined)

        def forward_rest(kept_pair):
            return (jnp.zeros_like(source), kept_pair[0], kept_pair[1])

        result, kept_inputs, kept_joined = lax.cond(
            active, forward_run, forward_rest, (kept_inputs, kept_joined)
        )
        return (pass_forward(result), kept_inputs, kept_joined)

    start_state = (
        jnp.zeros((per_group, length, model_width), jnp.bfloat16),
        jnp.zeros((micro_count, per_group, length, model_width), jnp.bfloat16),
        jnp.zeros(keep_shape, jnp.bfloat16),
    )
    _, kept_inputs, kept_joined = lax.fori_loop(0, step_count, forward_step, start_state)

    def backward_step(step_now, state_now):
        incoming, stores = state_now
        slot_index = step_now - (sections - 1 - section_index)
        active = jnp.logical_and(slot_index >= 0, slot_index < micro_count)
        group_index = jnp.clip(slot_index, 0, micro_count - 1)
        upstream = jnp.where(section_index == sections - 1, upstreams[group_index], incoming)

        def backward_run(store_now):
            source = kept_inputs[group_index]
            joined_rows = kept_joined[group_index]
            down_grad, normed, grad_joined_rows, mixed_heads, gain_part = layer_backward(
                source, gain_row, joined_rows, full_joined, full_out, allowed[group_index], upstream
            )
            new_store = (
                lax.dynamic_update_index_in_dim(store_now[0], normed, group_index, 0),
                lax.dynamic_update_index_in_dim(store_now[1], grad_joined_rows, group_index, 0),
                lax.dynamic_update_index_in_dim(store_now[2], mixed_heads, group_index, 0),
                lax.dynamic_update_index_in_dim(store_now[3], upstream, group_index, 0),
                store_now[4] + gain_part,
            )
            return (down_grad, new_store)

        def backward_rest(store_now):
            return (jnp.zeros_like(upstream), store_now)

        down_grad, stores = lax.cond(active, backward_run, backward_rest, stores)
        return (pass_backward(down_grad), stores)

    empty_stores = (
        jnp.zeros((micro_count, per_group, length, model_width), jnp.bfloat16),
        jnp.zeros((micro_count, per_group, length, joined_width), jnp.bfloat16),
        jnp.zeros((micro_count, per_group, length, inner_width), jnp.bfloat16),
        jnp.zeros((micro_count, per_group, length, model_width), jnp.bfloat16),
        jnp.zeros((model_width,), jnp.float32),
    )
    start_back = (jnp.zeros((per_group, length, model_width), jnp.bfloat16), empty_stores)
    _, stores = lax.fori_loop(0, step_count, backward_step, start_back)
    rows_normed = stores[0].reshape(-1, model_width)
    rows_joined = stores[1].reshape(-1, joined_width)
    rows_mixed = stores[2].reshape(-1, inner_width)
    rows_upstream = stores[3].reshape(-1, model_width)
    over_rows = (((0,), (0,)), ((), ()))
    gain_total = jnp.sum(lax.all_gather(stores[4], "dp", axis=0), axis=0)
    all_upstream = lax.all_gather(rows_upstream, "dp", axis=0, tiled=True)
    all_joined = lax.all_gather(rows_joined, "dp", axis=0, tiled=True)
    grad_output = lax.dot_general(
        share_columns(rows_mixed), all_upstream, over_rows, preferred_element_type=jnp.float32
    )
    grad_joined = lax.dot_general(
        share_columns(rows_normed), all_joined, over_rows, preferred_element_type=jnp.float32
    )
    return (grad_joined[None], grad_output[None], gain_total[None])


def solution(mesh):
    return jax.shard_map(
        body,
        mesh=mesh,
        in_specs=(
            P(("groups", "dp"), None),
            P(("groups", "dp"), None),
            P(("groups", "dp"), None, None),
            P("section", None),
            P("section", "dp", None),
            P("section", "dp", None),
        ),
        out_specs=(
            P(("groups", "section"), "dp", None),
            P(("groups", "section"), "dp", None),
            P(("groups", "section"), None),
        ),
        check_vma=False,
    )
```

```python
import functools

import jax
import jax.numpy as jnp
from jax import lax
from jax.experimental import pallas as pl
from jax.experimental.pallas import tpu as pltpu
from jax.sharding import PartitionSpec as P

NUM_HEADS = 24
HEAD_DIM = 64
BLOCK_LEN = 16


EPSILON = 1e-05


def from_behind(value, axis, steps):
    count = lax.axis_size(axis)
    initial, last = (max(0, -steps), min(count, count - steps))
    return lax.ppermute(value, axis, [(source, source + steps) for source in range(initial, last)])


def allowed_tokens(links, block_len):
    count = links.shape[1]
    block_hits = links[:, :, :, None] == jnp.arange(count, dtype=jnp.int32)[None, None, None, :]
    blocks = jnp.any(block_hits, axis=2)
    return jnp.repeat(jnp.repeat(blocks, block_len, axis=1), block_len, axis=2)


def normalize(stream, gain_row):
    stream_wide = stream.astype(jnp.float32)
    inv_rms = lax.rsqrt(jnp.mean(stream_wide * stream_wide, axis=-1, keepdims=True) + EPSILON)
    normed = (stream_wide * inv_rms * gain_row).astype(jnp.bfloat16)
    return (stream_wide, inv_rms, normed)


def project(normed, weight):
    batch_size, length, model_width = normed.shape
    flat = jnp.dot(normed.reshape(-1, model_width), weight, preferred_element_type=jnp.float32)
    return flat.astype(jnp.bfloat16).reshape(batch_size, length, weight.shape[1])


def attend(joined_rows, allowed):
    batch_size, length, _ = joined_rows.shape
    inner_width = NUM_HEADS * HEAD_DIM
    queries = joined_rows[:, :, :inner_width].reshape(batch_size, length, NUM_HEADS, HEAD_DIM)
    key_rows = joined_rows[:, :, inner_width : inner_width + HEAD_DIM]
    values = joined_rows[:, :, inner_width + HEAD_DIM :]
    scores = jnp.einsum(
        "bihd,bjd->bhij", queries, key_rows, preferred_element_type=jnp.float32
    ) * HEAD_DIM ** (-0.5)
    scores = jnp.where(allowed[:, None], scores, -1e30)
    row_max = jnp.max(scores, axis=-1, keepdims=True)
    exp_scores = jnp.exp(scores - row_max)
    attn_probs = exp_scores / jnp.sum(exp_scores, axis=-1, keepdims=True)
    probs_half = attn_probs.astype(jnp.bfloat16)
    mixed_heads = jnp.einsum(
        "bhij,bjd->bihd", probs_half, values, preferred_element_type=jnp.float32
    )
    mixed_heads = mixed_heads.astype(jnp.bfloat16).reshape(batch_size, length, inner_width)
    return (queries, key_rows, values, attn_probs, probs_half, mixed_heads)


def layer_forward(stream, gain_row, w_joined, w_out, allowed):
    stream_wide, inv_rms, normed = normalize(stream, gain_row)
    joined_rows = project(normed, w_joined)
    mixed_heads = attend(joined_rows, allowed)[5]
    batch_size, length, model_width = stream.shape
    update = jnp.dot(
        mixed_heads.reshape(-1, mixed_heads.shape[2]), w_out, preferred_element_type=jnp.float32
    )
    result = (stream_wide + update.reshape(batch_size, length, model_width)).astype(jnp.bfloat16)
    return (result, joined_rows)


def layer_backward(stream, gain_row, joined_rows, w_joined, w_out, allowed, upstream):
    stream_wide, inv_rms, normed = normalize(stream, gain_row)
    queries, key_rows, values, attn_probs, probs_half, mixed_heads = attend(joined_rows, allowed)
    batch_size, length, model_width = stream.shape
    inner_width = NUM_HEADS * HEAD_DIM
    grad_mixed = lax.dot_general(
        upstream.reshape(-1, model_width),
        w_out,
        (((1,), (1,)), ((), ())),
        preferred_element_type=jnp.float32,
    )
    grad_mixed = grad_mixed.astype(jnp.bfloat16).reshape(batch_size, length, NUM_HEADS, HEAD_DIM)
    grad_probs = jnp.einsum(
        "bihd,bjd->bhij", grad_mixed, values, preferred_element_type=jnp.float32
    )
    grad_values = jnp.einsum(
        "bhij,bihd->bjd", probs_half, grad_mixed, preferred_element_type=jnp.float32
    )
    inner_sum = jnp.sum(attn_probs * grad_probs, axis=-1, keepdims=True)
    grad_scores = (attn_probs * (grad_probs - inner_sum) * HEAD_DIM ** (-0.5)).astype(jnp.bfloat16)
    grad_queries = jnp.einsum(
        "bhij,bjd->bihd", grad_scores, key_rows, preferred_element_type=jnp.float32
    )
    grad_keys = jnp.einsum(
        "bhij,bihd->bjd", grad_scores, queries, preferred_element_type=jnp.float32
    )
    grad_joined_rows = jnp.concatenate(
        [grad_queries.reshape(batch_size, length, inner_width), grad_keys, grad_values], axis=-1
    ).astype(jnp.bfloat16)
    grad_normed = lax.dot_general(
        grad_joined_rows.reshape(-1, grad_joined_rows.shape[2]),
        w_joined,
        (((1,), (1,)), ((), ())),
        preferred_element_type=jnp.float32,
    )
    grad_normed = grad_normed.reshape(batch_size, length, model_width)
    gained = grad_normed * gain_row
    grad_stream = inv_rms * gained - stream_wide * inv_rms**3 * jnp.mean(
        stream_wide * gained, axis=-1, keepdims=True
    )
    down_grad = (upstream.astype(jnp.float32) + grad_stream).astype(jnp.bfloat16)
    gain_part = jnp.sum((grad_normed * stream_wide * inv_rms).reshape(-1, model_width), axis=0)
    return (down_grad, normed, grad_joined_rows, mixed_heads, gain_part)


def pass_forward(values):
    return from_behind(values, "section", 1)


def pass_backward(values):
    return from_behind(values, "section", -1)


CORES = 2
CHUNKS = 4


def gather_kernel(chips, groups, joined_ref, out_ref, full_joined, full_out, held_joined, held_out, *sems):
    load_sems, store_sems, send_x, recv_x, send_y, recv_y, send_own, recv_own, send_c, recv_c = sems
    me = lax.axis_index("dp")
    chip, core = me // CORES, lax.rem(me, CORES)
    group = lax.axis_index("groups")
    sibling = me + 1 - 2 * core
    pairs = ((joined_ref, full_joined), (out_ref, full_out))
    held = (held_joined, held_out)
    loads = [
        pltpu.make_async_copy(pairs[w][0], held[w], load_sems.at[w]) for w in range(2)
    ]
    for copy in loads:
        copy.start()

    barrier = pltpu.get_barrier_semaphore()
    partners = [{"dp": sibling}]
    partners += [{"dp": lax.rem(chip + k, chips) * CORES + core} for k in range(1, chips)]
    partners += [{"groups": lax.rem(group + g, groups)} for g in range(1, groups)]
    for partner in partners:
        pl.semaphore_signal(
            barrier, inc=1, device_id=partner, device_id_type=pl.DeviceIdType.MESH
        )
    pl.semaphore_wait(barrier, len(partners))

    def remote(src, dst, send_sem, recv_sem, partner):
        return pltpu.make_async_remote_copy(
            src_ref=src,
            dst_ref=dst,
            send_sem=send_sem,
            recv_sem=recv_sem,
            device_id=partner,
            device_id_type=pl.DeviceIdType.MESH,
        )

    def span(w, owner, part, chunk):
        rows = pairs[w][0].shape[0]
        size = rows // (groups * CHUNKS)
        inside = (part * CHUNKS + chunk) * size
        return pl.ds(inside, size), pl.ds(owner * rows + inside, size)

    first = {}
    for w, (mine, full) in enumerate(pairs):
        for chunk in range(CHUNKS):
            for k in range(1, chips):
                here, there = span(w, me, group, chunk)
                copy = remote(
                    mine.at[here],
                    full.at[there],
                    send_x.at[w, chunk, k - 1],
                    recv_x.at[w, chunk, k - 1],
                    partners[k],
                )
                copy.start()
                first[w, chunk, k] = copy
    own, local = [], []
    for w, (mine, full) in enumerate(pairs):
        rows = mine.shape[0]
        place = full.at[pl.ds(me * rows, rows)]
        own.append(remote(mine, place, send_own.at[w], recv_own.at[w], partners[0]))
        own[-1].start()
        loads[w].wait()
        local.append(pltpu.make_async_copy(held[w], place, store_sems.at[w]))
        local[-1].start()

    second, third = {}, []
    order = [
        (w, chunk, k) for w in range(2) for chunk in range(CHUNKS) for k in range(1, chips)
    ]

    def hand_over(w, chunk, k):
        owner = lax.rem(chip + chips - k, chips) * CORES + core
        for g in range(1, groups):
            second[w, chunk, k, g].wait_recv()
            part = lax.rem(group + groups - g, groups)
            _, place = span(w, owner, part, chunk)
            copy = remote(
                pairs[w][1].at[place],
                pairs[w][1].at[place],
                send_c.at[w, chunk, k - 1, g],
                recv_c.at[w, chunk, k - 1, g],
                partners[0],
            )
            copy.start()
            third.append(copy)

    for at, (w, chunk, k) in enumerate(order):
        first[w, chunk, k].wait_recv()
        owner = lax.rem(chip + chips - k, chips) * CORES + core
        _, place = span(w, owner, group, chunk)
        block = pairs[w][1].at[place]
        for g in range(1, groups):
            copy = remote(
                block,
                block,
                send_y.at[w, chunk, k - 1, g - 1],
                recv_y.at[w, chunk, k - 1, g - 1],
                partners[chips - 1 + g],
            )
            copy.start()
            second[w, chunk, k, g] = copy
        copy = remote(
            block,
            block,
            send_c.at[w, chunk, k - 1, 0],
            recv_c.at[w, chunk, k - 1, 0],
            partners[0],
        )
        copy.start()
        third.append(copy)
        if at:
            hand_over(*order[at - 1])
    hand_over(*order[-1])

    for copy in local:
        copy.wait()
    for copy in own:
        copy.wait()
    for copy in first.values():
        copy.wait_send()
    for copy in second.values():
        copy.wait_send()
    for copy in third:
        copy.wait()


def gather_weights(w_joined, w_out):
    replicas = lax.axis_size("dp")
    chips, groups = replicas // CORES, lax.axis_size("groups")
    shards = (w_joined[0], w_out[0])
    x_shape = (2, CHUNKS, chips - 1)
    dma = pltpu.SemaphoreType.DMA
    anywhere = pl.BlockSpec(memory_space=pl.ANY)
    return pl.pallas_call(
        functools.partial(gather_kernel, chips, groups),
        out_shape=[
            jax.ShapeDtypeStruct((replicas * each.shape[0], each.shape[1]), each.dtype)
            for each in shards
        ],
        in_specs=[anywhere] * 2,
        out_specs=[anywhere] * 2,
        scratch_shapes=[pltpu.VMEM(each.shape, each.dtype) for each in shards]
        + [dma((2,)), dma((2,)), dma(x_shape), dma(x_shape)]
        + [dma(x_shape + (groups - 1,))] * 2
        + [dma((2,))] * 2
        + [dma(x_shape + (groups,))] * 2,
        compiler_params=pltpu.CompilerParams(
            collective_id=0, has_side_effects=True, vmem_limit_bytes=16 << 20
        ),
    )(*shards)


def share_columns(rows):
    n = lax.axis_size("dp")
    me = lax.axis_index("dp")
    count, total = rows.shape
    width = total // n
    taken = jnp.zeros((n, count, width), rows.dtype)
    for shift in range(n):
        target = lax.rem(me + shift, n)
        piece = lax.dynamic_slice_in_dim(rows, target * width, width, 1)
        if shift:
            piece = lax.ppermute(piece, "dp", [(i, (i + shift) % n) for i in range(n)])
        source = lax.rem(me + n - shift, n)
        taken = lax.dynamic_update_slice_in_dim(taken, piece[None], source, 0)
    return taken.reshape(n * count, width)


def repeat(count, step, state):
    for now in range(count):
        state = step(now, state)
    return state


def body(stream_in, out_grad, mask_blocks, norm_gain, w_joined, w_out):
    full_joined, full_out = gather_weights(w_joined, w_out)
    gain_row = norm_gain[0]
    sections = lax.axis_size("section")
    section_index = lax.axis_index("section")
    micro_count = mask_blocks.shape[0]
    model_width = stream_in.shape[1]
    length = stream_in.shape[0] // micro_count
    joined_width = full_joined.shape[1]
    inner_width = full_out.shape[0]
    per_group = micro_count // micro_count
    inputs = stream_in.reshape(micro_count, per_group, length, model_width)
    upstreams = out_grad.reshape(micro_count, per_group, length, model_width)
    allowed = allowed_tokens(mask_blocks, BLOCK_LEN).reshape(micro_count, per_group, length, length)
    step_count = micro_count + sections - 1
    keep_shape = (micro_count + 1, per_group, length, joined_width)

    def forward_step(step_now, state_now):
        incoming, kept_inputs, kept_joined = state_now
        slot_index = step_now - section_index
        active = jnp.logical_and(slot_index >= 0, slot_index < micro_count)
        group_index = jnp.clip(slot_index, 0, micro_count - 1)
        place = jnp.where(active, group_index, micro_count)
        source = jnp.where(section_index == 0, inputs[group_index], incoming)

        def forward_run(kept_pair):
            result, joined_rows = layer_forward(
                source, gain_row, full_joined, full_out, allowed[group_index]
            )
            new_inputs = lax.dynamic_update_index_in_dim(kept_pair[0], source, place, 0)
            new_joined = lax.dynamic_update_index_in_dim(kept_pair[1], joined_rows, place, 0)
            return (result, new_inputs, new_joined)

        result, kept_inputs, kept_joined = forward_run((kept_inputs, kept_joined))
        return (pass_forward(result), kept_inputs, kept_joined)

    start_state = (
        jnp.zeros((per_group, length, model_width), jnp.bfloat16),
        jnp.zeros((micro_count + 1, per_group, length, model_width), jnp.bfloat16),
        jnp.zeros(keep_shape, jnp.bfloat16),
    )
    _, kept_inputs, kept_joined = repeat(step_count, forward_step, start_state)

    def backward_step(step_now, state_now):
        incoming, stores = state_now
        slot_index = step_now - (sections - 1 - section_index)
        active = jnp.logical_and(slot_index >= 0, slot_index < micro_count)
        group_index = jnp.clip(slot_index, 0, micro_count - 1)
        place = jnp.where(active, group_index, micro_count)
        upstream = jnp.where(section_index == sections - 1, upstreams[group_index], incoming)

        def backward_run(store_now):
            source = kept_inputs[group_index]
            joined_rows = kept_joined[group_index]
            down_grad, normed, grad_joined_rows, mixed_heads, gain_part = layer_backward(
                source, gain_row, joined_rows, full_joined, full_out, allowed[group_index], upstream
            )
            new_store = (
                lax.dynamic_update_index_in_dim(store_now[0], normed, place, 0),
                lax.dynamic_update_index_in_dim(store_now[1], grad_joined_rows, place, 0),
                lax.dynamic_update_index_in_dim(store_now[2], mixed_heads, place, 0),
                lax.dynamic_update_index_in_dim(store_now[3], upstream, place, 0),
                store_now[4] + jnp.where(active, gain_part, 0.0),
            )
            return (down_grad, new_store)

        down_grad, stores = backward_run(stores)
        return (pass_backward(down_grad), stores)

    empty_stores = (
        jnp.zeros((micro_count + 1, per_group, length, model_width), jnp.bfloat16),
        jnp.zeros((micro_count + 1, per_group, length, joined_width), jnp.bfloat16),
        jnp.zeros((micro_count + 1, per_group, length, inner_width), jnp.bfloat16),
        jnp.zeros((micro_count + 1, per_group, length, model_width), jnp.bfloat16),
        jnp.zeros((model_width,), jnp.float32),
    )
    start_back = (jnp.zeros((per_group, length, model_width), jnp.bfloat16), empty_stores)
    _, stores = repeat(step_count, backward_step, start_back)
    rows_normed = stores[0][:micro_count].reshape(-1, model_width)
    rows_joined = stores[1][:micro_count].reshape(-1, joined_width)
    rows_mixed = stores[2][:micro_count].reshape(-1, inner_width)
    rows_upstream = stores[3][:micro_count].reshape(-1, model_width)
    over_rows = (((0,), (0,)), ((), ()))
    gain_total = jnp.sum(lax.all_gather(stores[4], "dp", axis=0), axis=0)
    all_upstream = lax.all_gather(rows_upstream, "dp", axis=0, tiled=True)
    all_joined = lax.all_gather(rows_joined, "dp", axis=0, tiled=True)
    grad_output = lax.dot_general(
        share_columns(rows_mixed), all_upstream, over_rows, preferred_element_type=jnp.float32
    )
    grad_joined = lax.dot_general(
        share_columns(rows_normed), all_joined, over_rows, preferred_element_type=jnp.float32
    )
    return (grad_joined[None], grad_output[None], gain_total[None])


def solution(mesh):
    return jax.shard_map(
        body,
        mesh=mesh,
        in_specs=(
            P(("groups", "dp"), None),
            P(("groups", "dp"), None),
            P(("groups", "dp"), None, None),
            P("section", None),
            P("section", "dp", None),
            P("section", "dp", None),
        ),
        out_specs=(
            P(("groups", "section"), "dp", None),
            P(("groups", "section"), "dp", None),
            P(("groups", "section"), None),
        ),
        check_vma=False,
    )
```

```python
import functools

import jax
import jax.numpy as jnp
from jax import lax
from jax.experimental import pallas as pl
from jax.experimental.pallas import tpu as pltpu
from jax.sharding import PartitionSpec as P

NUM_HEADS = 24
HEAD_DIM = 64
BLOCK_LEN = 16


EPSILON = 1e-05


def from_behind(value, axis, steps):
    count = lax.axis_size(axis)
    initial, last = (max(0, -steps), min(count, count - steps))
    return lax.ppermute(value, axis, [(source, source + steps) for source in range(initial, last)])


def allowed_tokens(links, block_len):
    count = links.shape[1]
    block_hits = links[:, :, :, None] == jnp.arange(count, dtype=jnp.int32)[None, None, None, :]
    blocks = jnp.any(block_hits, axis=2)
    return jnp.repeat(jnp.repeat(blocks, block_len, axis=1), block_len, axis=2)


def normalize(stream, gain_row):
    stream_wide = stream.astype(jnp.float32)
    inv_rms = lax.rsqrt(jnp.mean(stream_wide * stream_wide, axis=-1, keepdims=True) + EPSILON)
    normed = (stream_wide * inv_rms * gain_row).astype(jnp.bfloat16)
    return (stream_wide, inv_rms, normed)


def project(normed, weight):
    batch_size, length, model_width = normed.shape
    flat = jnp.dot(normed.reshape(-1, model_width), weight, preferred_element_type=jnp.float32)
    return flat.astype(jnp.bfloat16).reshape(batch_size, length, weight.shape[1])


def attend(joined_rows, allowed):
    batch_size, length, _ = joined_rows.shape
    inner_width = NUM_HEADS * HEAD_DIM
    queries = joined_rows[:, :, :inner_width].reshape(batch_size, length, NUM_HEADS, HEAD_DIM)
    key_rows = joined_rows[:, :, inner_width : inner_width + HEAD_DIM]
    values = joined_rows[:, :, inner_width + HEAD_DIM :]
    scores = jnp.einsum(
        "bihd,bjd->bhij", queries, key_rows, preferred_element_type=jnp.float32
    ) * HEAD_DIM ** (-0.5)
    scores = jnp.where(allowed[:, None], scores, -1e30)
    row_max = jnp.max(scores, axis=-1, keepdims=True)
    exp_scores = jnp.exp(scores - row_max)
    attn_probs = exp_scores / jnp.sum(exp_scores, axis=-1, keepdims=True)
    probs_half = attn_probs.astype(jnp.bfloat16)
    mixed_heads = jnp.einsum(
        "bhij,bjd->bihd", probs_half, values, preferred_element_type=jnp.float32
    )
    mixed_heads = mixed_heads.astype(jnp.bfloat16).reshape(batch_size, length, inner_width)
    return (queries, key_rows, values, attn_probs, probs_half, mixed_heads)


def layer_forward(stream, gain_row, w_joined, w_out, allowed):
    stream_wide, inv_rms, normed = normalize(stream, gain_row)
    joined_rows = project(normed, w_joined)
    mixed_heads = attend(joined_rows, allowed)[5]
    batch_size, length, model_width = stream.shape
    update = jnp.dot(
        mixed_heads.reshape(-1, mixed_heads.shape[2]), w_out, preferred_element_type=jnp.float32
    )
    result = (stream_wide + update.reshape(batch_size, length, model_width)).astype(jnp.bfloat16)
    return (result, joined_rows)


def layer_backward(stream, gain_row, joined_rows, w_joined, w_out, allowed, upstream):
    stream_wide, inv_rms, normed = normalize(stream, gain_row)
    queries, key_rows, values, attn_probs, probs_half, mixed_heads = attend(joined_rows, allowed)
    batch_size, length, model_width = stream.shape
    inner_width = NUM_HEADS * HEAD_DIM
    grad_mixed = lax.dot_general(
        upstream.reshape(-1, model_width),
        w_out,
        (((1,), (1,)), ((), ())),
        preferred_element_type=jnp.float32,
    )
    grad_mixed = grad_mixed.astype(jnp.bfloat16).reshape(batch_size, length, NUM_HEADS, HEAD_DIM)
    grad_probs = jnp.einsum(
        "bihd,bjd->bhij", grad_mixed, values, preferred_element_type=jnp.float32
    )
    grad_values = jnp.einsum(
        "bhij,bihd->bjd", probs_half, grad_mixed, preferred_element_type=jnp.float32
    )
    inner_sum = jnp.sum(attn_probs * grad_probs, axis=-1, keepdims=True)
    grad_scores = (attn_probs * (grad_probs - inner_sum) * HEAD_DIM ** (-0.5)).astype(jnp.bfloat16)
    grad_queries = jnp.einsum(
        "bhij,bjd->bihd", grad_scores, key_rows, preferred_element_type=jnp.float32
    )
    grad_keys = jnp.einsum(
        "bhij,bihd->bjd", grad_scores, queries, preferred_element_type=jnp.float32
    )
    grad_joined_rows = jnp.concatenate(
        [grad_queries.reshape(batch_size, length, inner_width), grad_keys, grad_values], axis=-1
    ).astype(jnp.bfloat16)
    grad_normed = lax.dot_general(
        grad_joined_rows.reshape(-1, grad_joined_rows.shape[2]),
        w_joined,
        (((1,), (1,)), ((), ())),
        preferred_element_type=jnp.float32,
    )
    grad_normed = grad_normed.reshape(batch_size, length, model_width)
    gained = grad_normed * gain_row
    grad_stream = inv_rms * gained - stream_wide * inv_rms**3 * jnp.mean(
        stream_wide * gained, axis=-1, keepdims=True
    )
    down_grad = (upstream.astype(jnp.float32) + grad_stream).astype(jnp.bfloat16)
    gain_part = jnp.sum((grad_normed * stream_wide * inv_rms).reshape(-1, model_width), axis=0)
    return (down_grad, normed, grad_joined_rows, mixed_heads, gain_part)


def pass_forward(values):
    return from_behind(values, "section", 1)


def pass_backward(values):
    return from_behind(values, "section", -1)


CORES = 2
CHUNKS = 4


def gather_kernel(chips, groups, joined_ref, out_ref, full_joined, full_out, held_joined, held_out, *sems):
    load_sems, store_sems, send_x, recv_x, send_y, recv_y, send_own, recv_own, send_c, recv_c = sems
    me = lax.axis_index("dp")
    chip, core = me // CORES, lax.rem(me, CORES)
    group = lax.axis_index("groups")
    sibling = me + 1 - 2 * core
    pairs = ((joined_ref, full_joined), (out_ref, full_out))
    held = (held_joined, held_out)
    loads = [
        pltpu.make_async_copy(pairs[w][0], held[w], load_sems.at[w]) for w in range(2)
    ]
    for copy in loads:
        copy.start()

    barrier = pltpu.get_barrier_semaphore()
    partners = [{"dp": sibling}]
    partners += [{"dp": lax.rem(chip + k, chips) * CORES + core} for k in range(1, chips)]
    partners += [{"groups": lax.rem(group + g, groups)} for g in range(1, groups)]
    for partner in partners:
        pl.semaphore_signal(
            barrier, inc=1, device_id=partner, device_id_type=pl.DeviceIdType.MESH
        )
    pl.semaphore_wait(barrier, len(partners))

    def remote(src, dst, send_sem, recv_sem, partner):
        return pltpu.make_async_remote_copy(
            src_ref=src,
            dst_ref=dst,
            send_sem=send_sem,
            recv_sem=recv_sem,
            device_id=partner,
            device_id_type=pl.DeviceIdType.MESH,
        )

    def span(w, owner, part, chunk):
        rows = pairs[w][0].shape[0]
        size = rows // (groups * CHUNKS)
        inside = (part * CHUNKS + chunk) * size
        return pl.ds(inside, size), pl.ds(owner * rows + inside, size)

    first = {}
    for w, (mine, full) in enumerate(pairs):
        for chunk in range(CHUNKS):
            for k in range(1, chips):
                here, there = span(w, me, group, chunk)
                copy = remote(
                    mine.at[here],
                    full.at[there],
                    send_x.at[w, chunk, k - 1],
                    recv_x.at[w, chunk, k - 1],
                    partners[k],
                )
                copy.start()
                first[w, chunk, k] = copy
    own, local = [], []
    for w, (mine, full) in enumerate(pairs):
        rows = mine.shape[0]
        place = full.at[pl.ds(me * rows, rows)]
        own.append(remote(mine, place, send_own.at[w], recv_own.at[w], partners[0]))
        own[-1].start()
        loads[w].wait()
        local.append(pltpu.make_async_copy(held[w], place, store_sems.at[w]))
        local[-1].start()

    second, third = {}, []
    order = [
        (w, chunk, k) for w in range(2) for chunk in range(CHUNKS) for k in range(1, chips)
    ]

    def hand_over(w, chunk, k):
        owner = lax.rem(chip + chips - k, chips) * CORES + core
        for g in range(1, groups):
            second[w, chunk, k, g].wait_recv()
            part = lax.rem(group + groups - g, groups)
            _, place = span(w, owner, part, chunk)
            copy = remote(
                pairs[w][1].at[place],
                pairs[w][1].at[place],
                send_c.at[w, chunk, k - 1, g],
                recv_c.at[w, chunk, k - 1, g],
                partners[0],
            )
            copy.start()
            third.append(copy)

    for at, (w, chunk, k) in enumerate(order):
        first[w, chunk, k].wait_recv()
        owner = lax.rem(chip + chips - k, chips) * CORES + core
        _, place = span(w, owner, group, chunk)
        block = pairs[w][1].at[place]
        for g in range(1, groups):
            copy = remote(
                block,
                block,
                send_y.at[w, chunk, k - 1, g - 1],
                recv_y.at[w, chunk, k - 1, g - 1],
                partners[chips - 1 + g],
            )
            copy.start()
            second[w, chunk, k, g] = copy
        copy = remote(
            block,
            block,
            send_c.at[w, chunk, k - 1, 0],
            recv_c.at[w, chunk, k - 1, 0],
            partners[0],
        )
        copy.start()
        third.append(copy)
        if at:
            hand_over(*order[at - 1])
    hand_over(*order[-1])

    for copy in local:
        copy.wait()
    for copy in own:
        copy.wait()
    for copy in first.values():
        copy.wait_send()
    for copy in second.values():
        copy.wait_send()
    for copy in third:
        copy.wait()


def gather_weights(w_joined, w_out):
    replicas = lax.axis_size("dp")
    chips, groups = replicas // CORES, lax.axis_size("groups")
    shards = (w_joined[0], w_out[0])
    x_shape = (2, CHUNKS, chips - 1)
    dma = pltpu.SemaphoreType.DMA
    anywhere = pl.BlockSpec(memory_space=pl.ANY)
    return pl.pallas_call(
        functools.partial(gather_kernel, chips, groups),
        out_shape=[
            jax.ShapeDtypeStruct((replicas * each.shape[0], each.shape[1]), each.dtype)
            for each in shards
        ],
        in_specs=[anywhere] * 2,
        out_specs=[anywhere] * 2,
        scratch_shapes=[pltpu.VMEM(each.shape, each.dtype) for each in shards]
        + [dma((2,)), dma((2,)), dma(x_shape), dma(x_shape)]
        + [dma(x_shape + (groups - 1,))] * 2
        + [dma((2,))] * 2
        + [dma(x_shape + (groups,))] * 2,
        compiler_params=pltpu.CompilerParams(
            collective_id=0, has_side_effects=True, vmem_limit_bytes=16 << 20
        ),
    )(*shards)


def share_columns(rows):
    n = lax.axis_size("dp")
    me = lax.axis_index("dp")
    count, total = rows.shape
    width = total // n
    taken = jnp.zeros((n, count, width), rows.dtype)
    for shift in range(n):
        target = lax.rem(me + shift, n)
        piece = lax.dynamic_slice_in_dim(rows, target * width, width, 1)
        if shift:
            piece = lax.ppermute(piece, "dp", [(i, (i + shift) % n) for i in range(n)])
        source = lax.rem(me + n - shift, n)
        taken = lax.dynamic_update_slice_in_dim(taken, piece[None], source, 0)
    return taken.reshape(n * count, width)


def repeat(count, step, state):
    for now in range(count):
        state = step(now, state)
    return state


def body(stream_in, out_grad, mask_blocks, norm_gain, w_joined, w_out):
    full_joined, full_out = gather_weights(w_joined, w_out)
    gain_row = norm_gain[0]
    sections = lax.axis_size("section")
    section_index = lax.axis_index("section")
    micro_count = mask_blocks.shape[0]
    model_width = stream_in.shape[1]
    length = stream_in.shape[0] // micro_count
    joined_width = full_joined.shape[1]
    inner_width = full_out.shape[0]
    per_group = micro_count // micro_count
    inputs = stream_in.reshape(micro_count, per_group, length, model_width)
    upstreams = out_grad.reshape(micro_count, per_group, length, model_width)
    allowed = allowed_tokens(mask_blocks, BLOCK_LEN).reshape(micro_count, per_group, length, length)
    step_count = micro_count + sections - 1
    keep_shape = (micro_count + 1, per_group, length, joined_width)

    def forward_step(step_now, state_now):
        incoming, kept_inputs, kept_joined = state_now
        slot_index = step_now - section_index
        active = jnp.logical_and(slot_index >= 0, slot_index < micro_count)
        group_index = jnp.clip(slot_index, 0, micro_count - 1)
        place = jnp.where(active, group_index, micro_count)
        source = jnp.where(section_index == 0, inputs[group_index], incoming)

        def forward_run(kept_pair):
            result, joined_rows = layer_forward(
                source, gain_row, full_joined, full_out, allowed[group_index]
            )
            new_inputs = lax.dynamic_update_index_in_dim(kept_pair[0], source, place, 0)
            new_joined = lax.dynamic_update_index_in_dim(kept_pair[1], joined_rows, place, 0)
            return (result, new_inputs, new_joined)

        result, kept_inputs, kept_joined = forward_run((kept_inputs, kept_joined))
        return (pass_forward(result), kept_inputs, kept_joined)

    start_state = (
        jnp.zeros((per_group, length, model_width), jnp.bfloat16),
        jnp.zeros((micro_count + 1, per_group, length, model_width), jnp.bfloat16),
        jnp.zeros(keep_shape, jnp.bfloat16),
    )
    _, kept_inputs, kept_joined = repeat(step_count, forward_step, start_state)

    def backward_step(step_now, state_now):
        incoming, stores = state_now
        slot_index = step_now - (sections - 1 - section_index)
        active = jnp.logical_and(slot_index >= 0, slot_index < micro_count)
        group_index = jnp.clip(slot_index, 0, micro_count - 1)
        upstream = jnp.where(section_index == sections - 1, upstreams[group_index], incoming)

        def backward_run(store_now):
            source = kept_inputs[group_index]
            joined_rows = kept_joined[group_index]
            down_grad, normed, grad_joined_rows, mixed_heads, gain_part = layer_backward(
                source, gain_row, joined_rows, full_joined, full_out, allowed[group_index], upstream
            )
            new_store = (
                lax.dynamic_update_index_in_dim(store_now[0], normed, group_index, 0),
                lax.dynamic_update_index_in_dim(store_now[1], grad_joined_rows, group_index, 0),
                lax.dynamic_update_index_in_dim(store_now[2], mixed_heads, group_index, 0),
                lax.dynamic_update_index_in_dim(store_now[3], upstream, group_index, 0),
                store_now[4] + gain_part,
            )
            return (down_grad, new_store)

        def backward_rest(store_now):
            return (jnp.zeros_like(upstream), store_now)

        down_grad, stores = lax.cond(active, backward_run, backward_rest, stores)
        return (pass_backward(down_grad), stores)

    empty_stores = (
        jnp.zeros((micro_count, per_group, length, model_width), jnp.bfloat16),
        jnp.zeros((micro_count, per_group, length, joined_width), jnp.bfloat16),
        jnp.zeros((micro_count, per_group, length, inner_width), jnp.bfloat16),
        jnp.zeros((micro_count, per_group, length, model_width), jnp.bfloat16),
        jnp.zeros((model_width,), jnp.float32),
    )
    start_back = (jnp.zeros((per_group, length, model_width), jnp.bfloat16), empty_stores)
    _, stores = lax.fori_loop(0, step_count, backward_step, start_back)
    rows_normed = stores[0].reshape(-1, model_width)
    rows_joined = stores[1].reshape(-1, joined_width)
    rows_mixed = stores[2].reshape(-1, inner_width)
    rows_upstream = stores[3].reshape(-1, model_width)
    over_rows = (((0,), (0,)), ((), ()))
    gain_total = jnp.sum(lax.all_gather(stores[4], "dp", axis=0), axis=0)
    all_upstream = lax.all_gather(rows_upstream, "dp", axis=0, tiled=True)
    all_joined = lax.all_gather(rows_joined, "dp", axis=0, tiled=True)
    grad_output = lax.dot_general(
        share_columns(rows_mixed), all_upstream, over_rows, preferred_element_type=jnp.float32
    )
    grad_joined = lax.dot_general(
        share_columns(rows_normed), all_joined, over_rows, preferred_element_type=jnp.float32
    )
    return (grad_joined[None], grad_output[None], gain_total[None])


def solution(mesh):
    return jax.shard_map(
        body,
        mesh=mesh,
        in_specs=(
            P(("groups", "dp"), None),
            P(("groups", "dp"), None),
            P(("groups", "dp"), None, None),
            P("section", None),
            P("section", "dp", None),
            P("section", "dp", None),
        ),
        out_specs=(
            P(("groups", "section"), "dp", None),
            P(("groups", "section"), "dp", None),
            P(("groups", "section"), None),
        ),
        check_vma=False,
    )
```
